32 devices in a mesh: group: 2 (over y), seq: 4 (over z), exp: 2 (over x), tp: 2 (over core).
Axes of the slice: x: 2, y: 2, z: 4, core: 2. Of those that a mesh axis runs over, the one named last changes fastest.
Arguments:
- queries: bfloat16 [4, 512, 4096], P(('group', 'exp'), ('seq', 'tp')), parts along dimension 0, may hold values from -18 to 18
- keys_values: bfloat16 [4, 768, 2, 1024], P(('group', 'exp'), ('seq', 'tp')), parts along dimension 0, may hold values from -18 to 18
- prompt_lengths: int32 [4], P(('group', 'exp')), parts along dimension 0, may hold values from 1 to 256, 384 in all
- routes: int32 [4, 512, 8], P(('group', 'exp'), ('seq', 'tp')), parts along dimension 0, may hold values from 0 to 63, all different within a row; in each aligned block of 64 rows (0 to 63, 64 to 127, ..., all dimensions but the last counted through in order) at most 16 rows name the same one
- gate_weights: float32 [4, 512, 8], P(('group', 'exp'), ('seq', 'tp')), parts along dimension 0, may hold values from 0.05 to 0.5
- norm_gain: float32 [4096], replicated, may hold values from 0.5 to 1.5
- w_gate: bfloat16 [2, 4096, 2048], P('tp', None, 'seq'), may hold values from -0.09375 to 0.09375
- w_up: bfloat16 [2, 4096, 2048], P('tp', None, 'seq'), may hold values from -0.09375 to 0.09375
- w_down: bfloat16 [2, 2048, 4096], P('tp', 'seq'), may hold values from -0.125 to 0.125
Outputs:
- mixed: bfloat16 [4, 512, 4096], P(('group', 'exp'), ('seq', 'tp')), parts along dimension 0
The draws below stay inside these ranges and needn't reach their ends.
There are 2 independent parts, one for each index of `group`. The reference program is written for one: setup_inputs(seed, part) draws one part's arguments, and reference() takes and returns one part's arrays. A program takes and returns all parts, laid end to end along the dimension named above; an argument that names none is the same for every part. Nothing has to cross between parts.
Inputs may be any that keep to these rules, and one draw needn't show every extreme that they name: Each token's 8 routes name different experts. Among the 64 consecutive tokens of one device no expert is named by more than 16 tokens, a bound that some block reaches.
All inputs are finite; a program needn't handle non-finite values. No bound on the sum of `prompt_lengths` on one device may be relied on, other than what follows from the above.
Results may differ from the reference program's by a relative error of at most 0.02.
Values may be sent and summed in bfloat16 or wider, within the bound.
A program may use at most 128 MiB of HBM per device.

```python
import math
import jax
import jax.numpy as jnp
import numpy as np
from jax import lax

D = 4096
HEADS = 32
KV_HEADS = 8
HEAD_DIM = 128
EXPERTS = 64
TOP = 8
FF = 2048
PROMPT = 256
TOK_DEV = 64
IMAGES = 2
LEN = 512
KEYS = 768
WIN = 2
CAP = 16
N_SEQ = 4


def attention_pair(key):
    base_key = jax.random.fold_in(key, 7001)
    pair_width = KV_HEADS * HEAD_DIM
    pair_rows = jnp.clip(jax.random.normal(jax.random.fold_in(base_key, 1), (IMAGES, KEYS, 2, pair_width), jnp.float32), -3.0, 3.0)
    column_scale = jnp.exp(jax.random.uniform(jax.random.fold_in(base_key, 2), (pair_width,), jnp.float32, 0.0, math.log(10.0))) / 3.0
    query_rows = jnp.clip(jax.random.normal(jax.random.fold_in(base_key, 3), (IMAGES, LEN, HEADS * HEAD_DIM), jnp.float32), -3.0, 3.0)
    pair_rows = pair_rows.at[:, :, 1, :].multiply(column_scale)
    return (query_rows, pair_rows)


def draw_queries(key, part):
    return attention_pair(key)[0].astype(jnp.bfloat16)


def draw_keys_values(key, part):
    return attention_pair(key)[1].astype(jnp.bfloat16)


def levels(rng, extent, split, smallest, top_value):
    def one(dim, shards_of):
        steps = jax.random.uniform(jax.random.fold_in(jax.random.fold_in(rng, 6), dim), (shards_of,), jnp.float32, smallest / len(split), top_value / len(split))
        return jnp.repeat(jnp.exp(steps), extent[dim] // shards_of).reshape((-1,) + (1,) * (len(extent) - dim - 1))

    loudness = one(*split[0])
    for cut in split[1:]:
        loudness = loudness * one(*cut)
    return loudness


def split_up(amount, total, limit, lean):
    loads = [(1 << 20) // math.isqrt(grade ** lean) + 1 for grade in range(2, amount + 1)]
    rest, counts = total - limit - (amount - 1), [1] * (amount - 1)
    while rest > 0:
        free = [i for i in range(amount - 1) if counts[i] < limit]
        whole, budget = sum([loads[i] for i in free]), rest
        for i in free:
            addition = min(limit - counts[i], max(1, budget * loads[i] // whole), rest)
            counts[i] = counts[i] + addition
            rest = rest - addition
    return np.array([limit] + counts)


def ragged(key, number_of, total, reach, slope):
    if number_of == 2:
        one = jax.random.randint(key, (), max(1, total - reach), min(reach, total - 1) + 1)
        return jnp.stack([one, total - one])
    lengths = jnp.asarray(split_up(number_of, total, reach, slope), jnp.int32)
    couples = (number_of - 1) // 2
    donor, receiver = lengths[1:1 + 2 * couples:2], lengths[2:2 + 2 * couples:2]
    slack = jnp.minimum(donor - 1, reach - receiver)
    shifted = jax.random.randint(jax.random.fold_in(key, 1), (couples,), 0, 1 << 20) % (slack + 1)
    lengths = lengths.at[1:1 + 2 * couples:2].set(donor - shifted).at[2:2 + 2 * couples:2].set(receiver + shifted)
    return lengths[jax.random.permutation(jax.random.fold_in(key, 2), number_of)]


def assign_block(own_key, own, number, rows, number_of, top, limit, skew):
    ranking = jax.random.permutation(own_key, number_of)
    crowded, ordinary = portions_of(number_of, rows * top, limit, skew, True), portions_of(number_of, rows * top, limit, skew, False)
    places = jnp.arange(number_of)

    def named(tallies, rotation):
        used = int((tallies > 0).sum())
        fixed = max(1, used // 4)
        passed = fixed + (places - fixed + rotation * (used - fixed)) % max(1, number_of - fixed)
        return jnp.zeros((number_of,), jnp.int32).at[ranking[jnp.where(places < fixed, places, passed)]].set(jnp.asarray(tallies, jnp.int32))

    tallies = jnp.where(number % 4 == 0, named(crowded, number // 4), named(ordinary, number - number // 4 - 1))
    mixed = jax.random.permutation(jax.random.fold_in(own, 3), number_of)
    source_of, receiver = mixed[0:number_of // 2 * 2:2], mixed[1:number_of // 2 * 2:2]
    room = jnp.minimum(tallies[source_of] - 1, limit - tallies[receiver]) // 2
    room = jnp.where((source_of == ranking[0]) | (receiver == ranking[0]) | (tallies[receiver] == 0), 0, jnp.maximum(room, 0))
    passed = jax.random.randint(jax.random.fold_in(own, 4), (number_of // 2,), 0, 1 << 20) % (room + 1)
    tallies = tallies.at[source_of].add(-passed).at[receiver].add(passed)
    labels = jnp.searchsorted(jnp.cumsum(tallies), jnp.arange(rows * top), side="right").astype(jnp.int32)
    listing = labels.reshape(top, rows).T
    listing = listing[jax.random.permutation(jax.random.fold_in(own, 1), rows)]
    rotation = jax.random.randint(jax.random.fold_in(own, 2), (rows, 1), 0, top)
    return jnp.take_along_axis(listing, (jnp.arange(top)[None, :] + rotation) % top, axis=1)


def portions_of(amount, total, limit, slope, full):
    loads = [(1 << 20) // math.isqrt(grade ** slope) + 1 for grade in range(1, amount + 1)]
    largest = limit if full else min(limit, max(-(-total // amount), total * loads[0] // sum(loads)))
    least = 1 if total - largest >= amount - 1 else 0
    given, rest = [largest] + [least] * (amount - 1), total - largest - least * (amount - 1)
    while rest > 0:
        candidates = [i for i in range(1, amount) if given[i] < largest] or [i for i in range(1, amount) if given[i] < limit]
        mass, budget = sum([loads[i] for i in candidates]), rest
        for i in candidates:
            addition = min(limit - given[i], max(1, budget * loads[i] // mass), rest)
            given[i] = given[i] + addition
            rest = rest - addition
    return np.array(given)


def scatter_about(stream_key, shape, spread, limit, shards=(), dtype=jnp.bfloat16):
    values = jax.random.normal(stream_key, shape, jnp.float32) * spread
    if len(shards) > 0:
        values = levels(stream_key, shape, shards, -0.22, 0.18) * values
    return jnp.clip(values, min=-limit, max=limit).astype(dtype)


def setup_inputs(seed: int = 0, part: int = 0) -> dict:
    streams_of = jax.random.split(jax.random.key(seed), 10)
    own_keys = jax.random.split(jax.random.fold_in(streams_of[9], part), 10)
    queries = draw_queries(jax.random.fold_in(jax.random.fold_in(streams_of[9], part), 71), part)
    keys_values = draw_keys_values(jax.random.fold_in(jax.random.fold_in(streams_of[9], part), 71), part)
    prompt_lengths = ragged(own_keys[2], IMAGES, (IMAGES + 1) * PROMPT // 2, PROMPT, 0).astype(jnp.int32)
    routes_keys = jax.random.split(jax.random.fold_in(own_keys[3], 1), IMAGES * LEN // TOK_DEV)
    routes_turns = jax.random.permutation(jax.random.fold_in(own_keys[3], 3), IMAGES * LEN // TOK_DEV)
    routes = jax.vmap(lambda own, number: assign_block(jax.random.fold_in(own_keys[3], 2), own, number, TOK_DEV, EXPERTS, TOP, CAP, 2))(routes_keys, routes_turns).reshape((IMAGES, LEN, TOP))
    gate_weights = jnp.clip(jnp.exp(math.log(0.5) - 2.3025851 * jax.random.uniform(own_keys[4], (IMAGES, LEN, TOP), jnp.float32) ** levels(own_keys[4], (IMAGES, LEN, TOP), ((0, 2), (1, 8)), -0.2, 0.2)), 0.05, 0.5)
    norm_gain = jnp.clip(1.0 + 0.1 * jax.random.normal(streams_of[5], (D,), jnp.float32), 0.5, 1.5)
    w_gate = scatter_about(streams_of[6], (WIN, D, FF), D ** -0.5, 0.09375, ((0, 2), (2, 4)))
    w_up = scatter_about(streams_of[7], (WIN, D, FF), D ** -0.5, 0.09375, ((0, 2), (2, 4)))
    w_down = scatter_about(streams_of[8], (WIN, FF, D), FF ** -0.5, 0.125, ((0, 2), (1, 4)))
    return dict(queries=queries, keys_values=keys_values, prompt_lengths=prompt_lengths, routes=routes, gate_weights=gate_weights, norm_gain=norm_gain, w_gate=w_gate, w_up=w_up, w_down=w_down)


epsilon = 1e-06
masked_score = -1e+30

def rounded(values):
    return lax.optimization_barrier(values.astype(jnp.bfloat16)).astype(jnp.float32)

def attend_image(operands):
    queries_image, pairs_image, prompt_length = operands
    group = HEADS // KV_HEADS
    query_f = jnp.transpose(queries_image.astype(jnp.float32).reshape(LEN, KV_HEADS, group, HEAD_DIM), (1, 0, 2, 3))
    key_f = jnp.transpose(pairs_image[:, 0].astype(jnp.float32).reshape(KEYS, KV_HEADS, HEAD_DIM), (1, 0, 2))
    value_f = jnp.transpose(pairs_image[:, 1].astype(jnp.float32).reshape(KEYS, KV_HEADS, HEAD_DIM), (1, 0, 2))
    position = jnp.arange(KEYS).astype(jnp.int32)
    allowed = (position >= PROMPT) | (position < prompt_length)

    def one_head(pieces):
        query_head, key_head, value_head = pieces
        scores = jnp.einsum('lrd,kd->rlk', query_head, key_head) * (1.0 / math.sqrt(HEAD_DIM))
        scores = jnp.where(allowed, scores, masked_score)
        largest = lax.optimization_barrier(jnp.max(scores, axis=-1, keepdims=True))
        weights = jnp.where(allowed, jnp.exp(scores - largest), 0.0)
        totals = lax.optimization_barrier(jnp.sum(weights, axis=-1))
        summed = jnp.einsum('rlk,kd->lrd', rounded(weights), value_head)
        return summed / jnp.transpose(totals)[..., None]
    result = lax.map(one_head, (query_f, key_f, value_f))
    return jnp.transpose(result, (1, 0, 2, 3)).reshape(LEN, D).astype(jnp.bfloat16)

def reference(queries, keys_values, prompt_lengths, routes, gate_weights, norm_gain, w_gate, w_up, w_down):
    attended = lax.map(attend_image, (queries, keys_values, prompt_lengths))
    token_count = IMAGES * LEN
    flat_attended = attended.reshape(token_count, D).astype(jnp.float32)
    mean_square = lax.optimization_barrier(jnp.mean(flat_attended * flat_attended, axis=-1, keepdims=True))
    normed = (flat_attended * lax.rsqrt(mean_square + epsilon) * norm_gain).astype(jnp.bfloat16)
    route_ids = routes.reshape(token_count, TOP)
    route_gates = gate_weights.reshape(token_count, TOP)
    most_rows = token_count // TOK_DEV * CAP
    block_width = FF // N_SEQ
    combined = jnp.zeros((token_count, D), jnp.float32)
    for expert in range(WIN):
        hits = route_ids == expert
        member = jnp.any(hits, axis=1)
        weight = lax.optimization_barrier(jnp.sum(jnp.where(hits, route_gates, 0.0), axis=1))
        positions = jnp.nonzero(member, size=most_rows, fill_value=0)[0].astype(jnp.int32)
        filled = jnp.arange(most_rows) < jnp.sum(member.astype(jnp.int32))
        rows = normed[positions]
        gate_part = jnp.dot(rows, w_gate[expert], preferred_element_type=jnp.float32)
        up_part = jnp.dot(rows, w_up[expert], preferred_element_type=jnp.float32)
        hidden_units = (jax.nn.silu(gate_part) * up_part).astype(jnp.bfloat16)
        hidden_blocks = hidden_units.astype(jnp.float32).reshape(most_rows, N_SEQ, block_width)
        down_blocks = w_down[expert].astype(jnp.float32).reshape(N_SEQ, block_width, D)
        block_sums = rounded(jnp.einsum('rbf,bfd->rbd', hidden_blocks, down_blocks))
        expert_out = rounded(lax.optimization_barrier(jnp.sum(block_sums, axis=1)))
        scale_rows = jnp.where(filled, weight[positions], 0.0)
        combined = combined.at[positions].add(scale_rows[:, None] * expert_out)
    mixed = (flat_attended + combined).astype(jnp.bfloat16)
    return mixed.reshape(IMAGES, LEN, D)
```

```python
import functools
import math

import jax
import jax.numpy as jnp
from jax import lax
from jax.experimental import pallas as pl
from jax.experimental.pallas import tpu as pltpu
from jax.sharding import PartitionSpec as P

HEADS = 32
KV_HEADS = 8
HEAD_DIM = 128
PROMPT = 256
CAP = 16
LEAD = 4
SHIP = 5

epsilon = 1e-06
masked_score = -1e30
MESH = pl.DeviceIdType.MESH
F32 = jnp.float32
BF16 = jnp.bfloat16


def kernel(
    n, plen_ref, routes_hbm, gates_hbm, gain_hbm, kv_hbm, q_hbm, wg_hbm, wu_hbm, wd_hbm,
    out_ref,
    routes_ref, gates_ref, gain_ref, raw, q_ref, qx, ox, wg, wu, wd, kvbuf, att, sel, xsel, xbuf, part, rbuf, fin, ret,
    small_sem, w_sem, raw_sem, q_sem, kv_send, kv_recv, q_send, q_recv, o_send, o_recv,
    xs_send, xs_recv, x_send, x_recv, r_send, r_recv, y_send, y_recv,
):
    z = lax.axis_index("seq")
    c = lax.axis_index("tp")
    sib = 1 - c
    has_left = z > 0
    has_right = z < n - 1
    left, right, other = {"seq": z - 1}, {"seq": z + 1}, {"tp": sib}
    tokens = q_ref.shape[1]
    piece = raw.shape[1]
    groups = HEADS // KV_HEADS
    span = groups * HEAD_DIM
    width = KV_HEADS * span
    ff = wg.shape[1]
    two = 2
    keys = n * two * piece
    rows_here = two * CAP
    ship = SHIP if n >= 4 else 0

    is_end = (z == 0) | (z == n - 1)
    helps = (z == 1) | (z == n - 2)
    end = {"seq": jnp.where(z == 1, 0, n - 1)}
    helper = {"seq": jnp.where(z == 0, 1, n - 2)}

    barrier = pltpu.get_barrier_semaphore()

    @pl.when(has_left)
    def _():
        pl.semaphore_signal(barrier, inc=1, device_id=left, device_id_type=MESH)

    @pl.when(has_right)
    def _():
        pl.semaphore_signal(barrier, inc=1, device_id=right, device_id_type=MESH)

    pl.semaphore_signal(barrier, inc=1, device_id=other, device_id_type=MESH)

    own_kv = [
        pltpu.make_async_copy(
            kv_hbm.at[:, :, pl.ds(h * HEAD_DIM, HEAD_DIM)], raw.at[h], raw_sem.at[h]
        )
        for h in range(KV_HEADS)
    ]
    own_q = [
        pltpu.make_async_copy(q_hbm.at[:, pl.ds(h * span, span)], q_ref.at[h], q_sem.at[h])
        for h in range(KV_HEADS)
    ]
    small = [
        pltpu.make_async_copy(routes_hbm, routes_ref, small_sem.at[0]),
        pltpu.make_async_copy(gates_hbm, gates_ref, small_sem.at[1]),
        pltpu.make_async_copy(gain_hbm, gain_ref, small_sem.at[2]),
    ]
    loads = [
        pltpu.make_async_copy(wg_hbm, wg, w_sem.at[0]),
        pltpu.make_async_copy(wu_hbm, wu, w_sem.at[1]),
        pltpu.make_async_copy(wd_hbm, wd, w_sem.at[2]),
    ]
    for copy in own_kv + own_q + small:
        copy.start()

    row = lax.broadcasted_iota(jnp.int32, (two * piece, two * piece), 0)
    col = lax.broadcasted_iota(jnp.int32, (two * piece, two * piece), 1)
    source = jnp.where(row < piece, 2 * row, 2 * (row - piece) + 1)
    unzip = (col == source).astype(BF16)
    def remote(src, dst, send, recv, device):
        return pltpu.make_async_remote_copy(
            src_ref=src, dst_ref=dst, send_sem=send, recv_sem=recv,
            device_id=device, device_id_type=MESH,
        )

    def kv_copy(h, oz, oc, way, device):
        slot = kvbuf.at[h, :, oz, oc]
        return remote(slot, slot, kv_send.at[h, oz, way], kv_recv.at[h, oz, oc], device)

    def gathers(h):
        return jnp.logical_not(is_end & (h < ship))

    def goes_left(h):
        return has_left & jnp.logical_not((z == 1) & (h < ship))

    def goes_right(h):
        return has_right & jnp.logical_not((z == n - 2) & (h < ship))

    def query_copy(h):
        return remote(q_ref.at[h], qx.at[h], q_send.at[h], q_recv.at[h], helper)

    def answer_copy(h):
        return remote(ox.at[h], att.at[h], o_send.at[h], o_recv.at[h], end)

    def send_own(h):
        @pl.when(goes_left(h))
        def _():
            kv_copy(h, z, c, 0, left).start()

        @pl.when(goes_right(h))
        def _():
            kv_copy(h, z, c, 1, right).start()

        @pl.when(gathers(h))
        def _():
            kv_copy(h, z, c, 2, other).start()

        if ship:
            @pl.when(is_end & (h < ship))
            def _():
                query_copy(h).start()

    pl.semaphore_wait(barrier, 1 + has_left.astype(jnp.int32) + has_right.astype(jnp.int32))
    for h in range(KV_HEADS):
        own_kv[h].wait()
        own_q[h].wait()
        pairs = raw.at[h].reshape(two * piece, HEAD_DIM)[...]
        parted = jnp.dot(unzip, pairs, preferred_element_type=F32).astype(BF16)
        kvbuf[h, 0, z, c] = parted[:piece]
        kvbuf[h, 1, z, c] = parted[piece:]
        if 1 <= h <= LEAD:
            send_own(h - 1)
    if LEAD == KV_HEADS:
        send_own(LEAD - 1)
    for load in loads:
        load.start()

    for copy in small:
        copy.wait()
    plen = plen_ref[0]
    position = lax.broadcasted_iota(jnp.int32, (1, keys), 1)
    allowed = (position >= PROMPT) | (position < plen)

    routes = routes_ref[...]
    gates = gates_ref[...]
    tri = (
        lax.broadcasted_iota(jnp.int32, (tokens, tokens), 0)
        <= lax.broadcasted_iota(jnp.int32, (tokens, tokens), 1)
    ).astype(F32)
    slots = lax.broadcasted_iota(jnp.int32, (CAP, tokens), 0).astype(F32)
    combine = []
    for e in range(two):
        same = routes == e
        hit = jnp.max(same.astype(F32), axis=0, keepdims=True)
        gate = jnp.sum(jnp.where(same, gates, 0.0), axis=0, keepdims=True)
        rank = jnp.dot(jnp.broadcast_to(hit, (CAP, tokens)), tri, preferred_element_type=F32)
        select = jnp.where((rank - 1.0 == slots) & (hit > 0.0), 1.0, 0.0)
        combine.append(select * gate)
        sel[pl.ds(e * CAP, CAP), :] = select.astype(BF16)

    def attend(h, source, target):
        query = jnp.concatenate(
            [source[h, :, g * HEAD_DIM:(g + 1) * HEAD_DIM] for g in range(groups)], axis=0
        )
        key_rows = kvbuf[h, 0].reshape(keys, HEAD_DIM)
        value_rows = kvbuf[h, 1].reshape(keys, HEAD_DIM)
        scores = lax.dot_general(
            query, key_rows, (((1,), (1,)), ((), ())), preferred_element_type=F32
        ) * (1.0 / math.sqrt(HEAD_DIM))
        scores = jnp.where(allowed, scores, masked_score)
        weights = jnp.exp(scores - jnp.max(scores, axis=1, keepdims=True))
        total = jnp.sum(weights, axis=1, keepdims=True)
        summed = jnp.dot(weights.astype(BF16), value_rows, preferred_element_type=F32)
        result = (summed / total).astype(BF16)
        for g in range(groups):
            target[h, :, g * HEAD_DIM:(g + 1) * HEAD_DIM] = result[g * tokens:(g + 1) * tokens]

    def row_copy(oz, h, way, device):
        slot = xbuf.at[oz, h]
        return remote(slot, slot, x_send.at[oz, h, way], x_recv.at[oz, h], device)

    def sib_copy(h):
        return remote(xsel.at[h, sib], xbuf.at[z, h, c], xs_send.at[h], xs_recv.at[h], other)

    reach = jnp.maximum(z, n - 1 - z)

    def kv_round(r, carry):
        @pl.when(r + LEAD < KV_HEADS)
        def _():
            send_own(r + LEAD)

        for d in range(1, n):
            h = r - (d - 1)
            live = (h >= 0) & (h < KV_HEADS) & gathers(h)

            @pl.when(live & (z - d >= 0))
            def _():
                kv_copy(h, z - d, c, 2, other).wait_recv()

                @pl.when(goes_right(h))
                def _():
                    kv_copy(h, z - d, c, 1, right).start()

                kv_copy(h, z - d, c, 2, other).start()

            @pl.when(live & (z + d < n))
            def _():
                kv_copy(h, z + d, c, 2, other).wait_recv()

                @pl.when(goes_left(h))
                def _():
                    kv_copy(h, z + d, c, 0, left).start()

                kv_copy(h, z + d, c, 2, other).start()

        passed = r - reach - 2

        @pl.when((passed >= 0) & (passed < KV_HEADS))
        def _():
            sib_copy(passed).wait_recv()

            @pl.when(has_left)
            def _():
                row_copy(z, passed, 0, left).start()

            @pl.when(has_right)
            def _():
                row_copy(z, passed, 1, right).start()

        chosen = r - reach - 1

        @pl.when((chosen >= 0) & (chosen < KV_HEADS))
        def _():
            if ship:
                @pl.when(is_end & (chosen < ship))
                def _():
                    answer_copy(chosen).wait_recv()

            picked = jnp.dot(sel[...], att[chosen], preferred_element_type=F32).astype(BF16)
            xsel[chosen] = picked.reshape(two, CAP, span)
            xbuf[z, chosen, c] = xsel[chosen, c]
            sib_copy(chosen).start()

        done = r - reach

        @pl.when((done >= 0) & (done < KV_HEADS) & gathers(done))
        def _():
            for oz in range(n):
                kv_copy(done, oz, sib, 2, other).wait_recv()

            if ship:
                @pl.when(helps & (done < ship))
                def _():
                    query_copy(done).wait_recv()
                    attend(done, qx, ox)
                    answer_copy(done).start()

            attend(done, q_ref, att)

        return carry

    lax.fori_loop(0, KV_HEADS + n + 1, kv_round, 0)

    for load in loads:
        load.wait()

    def sum_copy(way, dest, k, device):
        return remote(
            part.at[dest, k], rbuf.at[way, dest, k], r_send.at[way, dest, k], r_recv.at[way, dest, k],
            device,
        )

    def expert(origins, arrive, leave):
        count = len(origins)
        gate_part = jnp.zeros((count * rows_here, ff), F32)
        up_part = jnp.zeros((count * rows_here, ff), F32)
        squares = jnp.zeros((count * rows_here, 1), F32)
        for h in range(KV_HEADS):
            cols = slice(h * span, (h + 1) * span)
            arrive(h)
            rows = jnp.concatenate(
                [xbuf[origin, h].reshape(rows_here, span) for origin in origins], axis=0
            ).astype(F32)
            squares += jnp.sum(rows * rows, axis=1, keepdims=True)
            scaled = (rows * gain_ref[:, cols]).astype(BF16)
            gate_part += jnp.dot(scaled, wg[cols, :], preferred_element_type=F32)
            up_part += jnp.dot(scaled, wu[cols, :], preferred_element_type=F32)
        inverse = lax.rsqrt(squares * (1.0 / width) + epsilon)
        gate_part *= inverse
        up_part *= inverse
        hidden = (gate_part / (1.0 + jnp.exp(-gate_part)) * up_part).astype(BF16)
        for k in range(KV_HEADS):
            cols = slice(k * span, (k + 1) * span)
            block = jnp.dot(hidden, wd[:, cols], preferred_element_type=F32).astype(BF16)
            for i, origin in enumerate(origins):
                part[origin, k] = block[i * rows_here:(i + 1) * rows_here]
            leave(k)

    def take_from_left(oz, h):
        row_copy(oz, h, 1, right).wait_recv()

        @pl.when(has_right)
        def _():
            row_copy(oz, h, 1, right).start()

    def take_from_right(oz, h):
        row_copy(oz, h, 0, left).wait_recv()

        @pl.when(has_left)
        def _():
            row_copy(oz, h, 0, left).start()

    def start_sum(origin, k):
        @pl.when(z == 0)
        def _():
            sum_copy(0, origin, k, right).start()

        @pl.when(z == n - 1)
        def _():
            sum_copy(1, origin, k, left).start()

    def single(t, with_own):
        from_left = z - t >= 0
        origin = jnp.where(from_left, z - t, z + t)

        def arrive(h):
            @pl.when(from_left)
            def _():
                take_from_left(z - t, h)

            @pl.when(jnp.logical_not(from_left))
            def _():
                take_from_right(z + t, h)

        expert([origin, z] if with_own else [origin], arrive, lambda k: start_sum(origin, k))

    def near(h):
        take_from_left(z - 1, h)
        take_from_right(z + 1, h)

    @pl.when(is_end)
    def _():
        single(1, True)

    @pl.when(jnp.logical_not(is_end))
    def _():
        expert([z - 1, z + 1, z], near, lambda k: None)

    def pass_sum(way, dest, device):
        for k in range(KV_HEADS):
            sum_copy(way, dest, k, device).wait_recv()
            part[dest, k] = (part[dest, k].astype(F32) + rbuf[way, dest, k].astype(F32)).astype(BF16)
            sum_copy(way, dest, k, device).start()

    def expert_round(t, carry):
        def side(k, inner):
            origin = jnp.where(k == 0, z - t, z + t)

            @pl.when((origin >= 0) & (origin < n))
            def _():
                def arrive(h):
                    @pl.when(k == 0)
                    def _():
                        take_from_left(origin, h)

                    @pl.when(k == 1)
                    def _():
                        take_from_right(origin, h)

                expert([origin], arrive, lambda k: start_sum(origin, k))

            return inner

        lax.fori_loop(0, 2, side, 0)

        dest = t - z

        @pl.when(has_left & (dest > z) & (dest < n))
        def _():
            pass_sum(0, dest, right)

        mirror = n - 1 - z
        back = t - mirror
        home = n - 1 - back

        @pl.when(has_right & (back > mirror) & (back < n))
        def _():
            pass_sum(1, home, left)

        return carry

    lax.fori_loop(2, 2 * n - 2, expert_round, 0)

    def result_copy(oc, k):
        return remote(fin.at[k, sib], ret.at[oc, k], y_send.at[k], y_recv.at[k], other)

    for k in range(KV_HEADS):
        @pl.when(has_left)
        def _():
            sum_copy(0, z, k, right).wait_recv()

        @pl.when(has_right)
        def _():
            sum_copy(1, z, k, left).wait_recv()

        own = part[z, k].astype(F32)
        own += jnp.where(has_left, rbuf[0, z, k].astype(F32), 0.0)
        own += jnp.where(has_right, rbuf[1, z, k].astype(F32), 0.0)
        fin[k] = own.astype(BF16).reshape(two, CAP, span)
        result_copy(c, k).start()
        ret[c, k] = fin[k, c]

    cw = jnp.transpose(jnp.concatenate(combine, axis=0))
    first = cw.astype(BF16)
    rest = cw - first.astype(F32)
    second = rest.astype(BF16)
    third = (rest - second.astype(F32)).astype(BF16)
    for k in range(KV_HEADS):
        cols = slice(k * span, (k + 1) * span)
        result_copy(sib, k).wait_recv()
        returned = ret[:, k].reshape(rows_here, span)
        total = (
            jnp.dot(first, returned, preferred_element_type=F32)
            + jnp.dot(second, returned, preferred_element_type=F32)
            + jnp.dot(third, returned, preferred_element_type=F32)
        )
        out_ref[:, cols] = (att[k].astype(F32) + total).astype(BF16)

    def drain(h, carry):
        result_copy(c, h).wait_send()
        sib_copy(h).wait_send()
        if ship:
            @pl.when(is_end & (h < ship))
            def _():
                query_copy(h).wait_send()

            @pl.when(helps & (h < ship))
            def _():
                answer_copy(h).wait_send()

        for oz in range(n):
            @pl.when(goes_left(h) & (oz >= z))
            def _():
                kv_copy(h, oz, c, 0, left).wait_send()

            @pl.when(goes_right(h) & (oz <= z))
            def _():
                kv_copy(h, oz, c, 1, right).wait_send()

            @pl.when(gathers(h))
            def _():
                kv_copy(h, oz, c, 2, other).wait_send()

            @pl.when(has_left & (oz >= z))
            def _():
                row_copy(oz, h, 0, left).wait_send()

            @pl.when(has_right & (oz <= z))
            def _():
                row_copy(oz, h, 1, right).wait_send()

            @pl.when(oz > z)
            def _():
                sum_copy(0, oz, h, right).wait_send()

            @pl.when(oz < z)
            def _():
                sum_copy(1, oz, h, left).wait_send()
        return carry

    lax.fori_loop(0, KV_HEADS, drain, 0)


def body(
    queries, keys_values, prompt_lengths, routes, gate_weights, norm_gain, w_gate, w_up, w_down
):
    n = lax.axis_size("seq")
    tokens, width = queries.shape[1:]
    piece = keys_values.shape[1]
    ff = w_gate.shape[2]
    span = width // KV_HEADS
    top = routes.shape[2]
    vmem = pl.BlockSpec(memory_space=pltpu.VMEM)
    hbm = pl.BlockSpec(memory_space=pltpu.HBM)
    dma = pltpu.SemaphoreType.DMA
    mixed = pl.pallas_call(
        functools.partial(kernel, n),
        out_shape=jax.ShapeDtypeStruct((tokens, width), BF16),
        in_specs=[pl.BlockSpec(memory_space=pltpu.SMEM)] + [hbm] * 8,
        out_specs=vmem,
        scratch_shapes=[
            pltpu.VMEM((top, tokens), jnp.int32),
            pltpu.VMEM((top, tokens), F32),
            pltpu.VMEM((1, width), F32),
            pltpu.VMEM((KV_HEADS, piece, 2, HEAD_DIM), BF16),
            pltpu.VMEM((KV_HEADS, tokens, span), BF16),
            pltpu.VMEM((KV_HEADS, tokens, span), BF16),
            pltpu.VMEM((KV_HEADS, tokens, span), BF16),
            pltpu.VMEM((width, ff), BF16),
            pltpu.VMEM((width, ff), BF16),
            pltpu.VMEM((ff, width), BF16),
            pltpu.VMEM((KV_HEADS, 2, n, 2, piece, HEAD_DIM), BF16),
            pltpu.VMEM((KV_HEADS, tokens, span), BF16),
            pltpu.VMEM((2 * CAP, tokens), BF16),
            pltpu.VMEM((KV_HEADS, 2, CAP, span), BF16),
            pltpu.VMEM((n, KV_HEADS, 2, CAP, span), BF16),
            pltpu.VMEM((n, KV_HEADS, 2 * CAP, span), BF16),
            pltpu.VMEM((2, n, KV_HEADS, 2 * CAP, span), BF16),
            pltpu.VMEM((KV_HEADS, 2, CAP, span), BF16),
            pltpu.VMEM((2, KV_HEADS, CAP, span), BF16),
            dma((3,)),
            dma((3,)),
            dma((KV_HEADS,)),
            dma((KV_HEADS,)),
            dma((KV_HEADS, n, 3)),
            dma((KV_HEADS, n, 2)),
            dma((KV_HEADS,)),
            dma((KV_HEADS,)),
            dma((KV_HEADS,)),
            dma((KV_HEADS,)),
            dma((KV_HEADS,)),
            dma((KV_HEADS,)),
            dma((n, KV_HEADS, 2)),
            dma((n, KV_HEADS)),
            dma((2, n, KV_HEADS)),
            dma((2, n, KV_HEADS)),
            dma((KV_HEADS,)),
            dma((KV_HEADS,)),
        ],
        compiler_params=pltpu.CompilerParams(
            collective_id=0, has_side_effects=True, vmem_limit_bytes=48 * 1024 * 1024
        ),
    )(
        prompt_lengths,
        *[
            pltpu.with_memory_space_constraint(operand, pltpu.HBM)
            for operand in (
                routes[0].T, gate_weights[0].T, norm_gain[None], keys_values[0], queries[0],
                w_gate[0], w_up[0], w_down[0],
            )
        ],
    )
    return mixed[None]


def solution(mesh):
    return jax.shard_map(
        body,
        mesh=mesh,
        in_specs=(
            P(("group", "exp"), ("seq", "tp"), None),
            P(("group", "exp"), ("seq", "tp"), None, None),
            P(("group", "exp")),
            P(("group", "exp"), ("seq", "tp"), None),
            P(("group", "exp"), ("seq", "tp"), None),
            P(),
            P("tp", None, "seq"),
            P("tp", None, "seq"),
            P("tp", "seq", None),
        ),
        out_specs=P(("group", "exp"), ("seq", "tp"), None),
        check_vma=False,
    )
```
